32 devices in a mesh: group: 4 (over y, x), fsdp: 4 (over z), tp: 2 (over core).
Axes of the slice: x: 2, y: 2, z: 4, core: 2. Of those that a mesh axis runs over, the one named last changes fastest.
Arguments:
- tokens: bfloat16 [4, 2048, 1152], P('group', ('fsdp', 'tp')), may hold values from -6 to 6
- layer_input: bfloat16 [4, 2048, 256], P('group', ('fsdp', 'tp')), may hold values from -6 to 6
- prefix_len: int32 [4], P('group'), may hold values from 0 to 2048
- out_grad: bfloat16 [4, 2048, 1152], P('group', ('fsdp', 'tp')), may hold values from -6 to 6
- w_attn: bfloat16 [1152, 2, 768], P('fsdp', 'tp'), may hold values from -0.1875 to 0.1875
- w_proj: bfloat16 [2, 512, 1152], P('tp', None, 'fsdp'), may hold values from -0.1875 to 0.1875
- w_gate: bfloat16 [1152, 2, 6912], P('fsdp', None, 'tp'), may hold values from -0.1875 to 0.1875
- w_down: bfloat16 [6912, 1152], P('tp', 'fsdp'), may hold values from -0.078125 to 0.078125
- w_left: bfloat16 [1152, 320], P('fsdp'), may hold values from -0.1875 to 0.1875
- w_right: bfloat16 [326, 1152], P(None, 'fsdp'), may hold values from -0.5 to 1.3
- w_norm: bfloat16 [2, 256], P(None, 'fsdp'), may hold values from 1 to 1.59375
- first_attn: float32 [4, 1152, 2, 768], P('group', 'fsdp', 'tp'), may hold values from -60 to 60
- second_attn: float32 [4, 1152, 2, 768], P('group', 'fsdp', 'tp'), may hold values from 100 to 1000
- drift_attn: float32 [1152, 2, 768], P('fsdp', 'tp'), may hold values from -0.06 to 0.06
- first_proj: float32 [4, 2, 512, 1152], P('group', 'tp', None, 'fsdp'), may hold values from -60 to 60
- second_proj: float32 [4, 2, 512, 1152], P('group', 'tp', None, 'fsdp'), may hold values from 100 to 1000
- drift_proj: float32 [2, 512, 1152], P('tp', None, 'fsdp'), may hold values from -0.06 to 0.06
- first_gate: float32 [4, 1152, 2, 6912], P('group', 'fsdp', None, 'tp'), may hold values from -60 to 60
- second_gate: float32 [4, 1152, 2, 6912], P('group', 'fsdp', None, 'tp'), may hold values from 2 to 25
- drift_gate: float32 [1152, 2, 6912], P('fsdp', None, 'tp'), may hold values from -0.06 to 0.06
- first_down: float32 [4, 6912, 1152], P('group', 'tp', 'fsdp'), may hold values from -60 to 60
- second_down: float32 [4, 6912, 1152], P('group', 'tp', 'fsdp'), may hold values from 100 to 1000
- drift_down: float32 [6912, 1152], P('tp', 'fsdp'), may hold values from -0.06 to 0.06
- first_left: float32 [4, 1152, 320], P('group', ('fsdp', 'tp')), may hold values from -60 to 60
- second_left: float32 [4, 1152, 320], P('group', ('fsdp', 'tp')), may hold values from 100 to 1000
- drift_left: float32 [1152, 320], P(('fsdp', 'tp')), may hold values from -0.06 to 0.06
- first_right: float32 [4, 326, 1152], P('group', None, ('fsdp', 'tp')), may hold values from -60 to 60
- second_right: float32 [4, 326, 1152], P('group', None, ('fsdp', 'tp')), may hold values from 100 to 1000
- drift_right: float32 [326, 1152], P(None, ('fsdp', 'tp')), may hold values from -0.06 to 0.06
- first_norm: float32 [4, 2, 256], P('group', None, ('fsdp', 'tp')), may hold values from -60 to 60
- second_norm: float32 [4, 2, 256], P('group', None, ('fsdp', 'tp')), may hold values from 100 to 1000
- drift_norm: float32 [2, 256], P(None, ('fsdp', 'tp')), may hold values from -0.06 to 0.06
Outputs:
- block_out: bfloat16 [4, 2048, 1152], P('group', ('fsdp', 'tp'))
- input_grad: float32 [4, 2048, 1152], P('group', ('fsdp', 'tp'))
- grad_attn: float32 [4, 1152, 2, 768], P('group', 'fsdp', 'tp')
- mean_attn: float32 [4, 1152, 2, 768], P('group', 'fsdp', 'tp')
- square_attn: float32 [4, 1152, 2, 768], P('group', 'fsdp', 'tp')
- delta_attn: float32 [1152, 2, 768], P('fsdp', 'tp')
- outer_attn: float32 [1152, 2, 768], P('fsdp', 'tp')
- master_attn: float32 [1152, 2, 768], P('fsdp', 'tp')
- grad_proj: float32 [4, 2, 512, 1152], P('group', 'tp', None, 'fsdp')
- mean_proj: float32 [4, 2, 512, 1152], P('group', 'tp', None, 'fsdp')
- square_proj: float32 [4, 2, 512, 1152], P('group', 'tp', None, 'fsdp')
- delta_proj: float32 [2, 512, 1152], P('tp', None, 'fsdp')
- outer_proj: float32 [2, 512, 1152], P('tp', None, 'fsdp')
- master_proj: float32 [2, 512, 1152], P('tp', None, 'fsdp')
- grad_gate: float32 [4, 1152, 2, 6912], P('group', 'fsdp', None, 'tp')
- mean_gate: float32 [4, 1152, 2, 6912], P('group', 'fsdp', None, 'tp')
- square_gate: float32 [4, 1152, 2, 6912], P('group', 'fsdp', None, 'tp')
- delta_gate: float32 [1152, 2, 6912], P('fsdp', None, 'tp')
- outer_gate: float32 [1152, 2, 6912], P('fsdp', None, 'tp')
- master_gate: float32 [1152, 2, 6912], P('fsdp', None, 'tp')
- grad_down: float32 [4, 6912, 1152], P('group', 'tp', 'fsdp')
- mean_down: float32 [4, 6912, 1152], P('group', 'tp', 'fsdp')
- square_down: float32 [4, 6912, 1152], P('group', 'tp', 'fsdp')
- delta_down: float32 [6912, 1152], P('tp', 'fsdp')
- outer_down: float32 [6912, 1152], P('tp', 'fsdp')
- master_down: float32 [6912, 1152], P('tp', 'fsdp')
- grad_left: float32 [4, 1152, 320], P('group', ('fsdp', 'tp'))
- mean_left: float32 [4, 1152, 320], P('group', ('fsdp', 'tp'))
- square_left: float32 [4, 1152, 320], P('group', ('fsdp', 'tp'))
- delta_left: float32 [1152, 320], P(('fsdp', 'tp'))
- outer_left: float32 [1152, 320], P(('fsdp', 'tp'))
- master_left: float32 [1152, 320], P(('fsdp', 'tp'))
- grad_right: float32 [4, 326, 1152], P('group', None, ('fsdp', 'tp'))
- mean_right: float32 [4, 326, 1152], P('group', None, ('fsdp', 'tp'))
- square_right: float32 [4, 326, 1152], P('group', None, ('fsdp', 'tp'))
- delta_right: float32 [326, 1152], P(None, ('fsdp', 'tp'))
- outer_right: float32 [326, 1152], P(None, ('fsdp', 'tp'))
- grad_norm: float32 [4, 2, 256], P('group', None, ('fsdp', 'tp'))
- mean_norm: float32 [4, 2, 256], P('group', None, ('fsdp', 'tp'))
- square_norm: float32 [4, 2, 256], P('group', None, ('fsdp', 'tp'))
- delta_norm: float32 [2, 256], P(None, ('fsdp', 'tp'))
- outer_norm: float32 [2, 256], P(None, ('fsdp', 'tp'))
The draws below stay inside these ranges and needn't reach their ends.
All inputs are finite; a program needn't handle non-finite values.
Results may differ from the reference program's by a relative error of at most 0.025.
Values may be sent and summed in bfloat16 or wider, within the bound.
No kernel may reach another device: no remote copies, remote signals or barrier semaphores. Data moves between devices by JAX's collectives and lax.ppermute only.
A program may use at most 216 MiB of HBM per device.

```python
import math
import jax
import jax.numpy as jnp
from jax import lax

D = 1152
HEADS = 4
HD = 256
FF = 6912
RANK = 64
PLI = 256
QPT = 2
SEQ = 2048
GROUPS = 4


def draw_w_right(key, part):
    key_one, key_two = jax.random.split(key)
    entries = jnp.clip(jax.random.normal(key_one, (RANK + PLI, D), jnp.float32), -4.0, 4.0)
    row_index = jnp.arange(RANK + PLI)
    row_scale = jnp.where(row_index < RANK, RANK ** (-0.5), PLI ** (-0.5)).astype(jnp.float32)
    scaled = jnp.clip(entries * row_scale[:, None], -0.5, 0.5)
    gain_rows = jax.random.uniform(key_two, (6, D), jnp.float32, 0.7, 1.3)
    return jnp.concatenate([scaled, gain_rows], axis=0).astype(jnp.bfloat16)


def touch_ends(array, key, low, top_value):
    place = [jax.random.randint(jax.random.fold_in(key, axis), (), 0, length) for axis, length in enumerate(array.shape)]
    longest = array.shape.index(max(array.shape))
    beside = place[:longest] + [(place[longest] + 1) % array.shape[longest]] + place[longest + 1:]
    return array.at[tuple(place)].set(low).at[tuple(beside)].set(top_value)


def block_levels(stream_key, dims, cuts, least, top_value):
    def one(position, parts):
        steps = jax.random.uniform(jax.random.fold_in(jax.random.fold_in(stream_key, 6), position), (parts,), jnp.float32, least / len(cuts), top_value / len(cuts))
        return jnp.repeat(jnp.exp(steps), dims[position] // parts).reshape((-1,) + (1,) * (len(dims) - position - 1))

    loudness = one(*cuts[0])
    for cut in cuts[1:]:
        loudness = loudness * one(*cut)
    return loudness


def normal_values(own_key, shape, spread, most, cuts=(), kind=jnp.bfloat16):
    loudness = block_levels(own_key, shape, cuts, -0.22, 0.18) if cuts else 1.0
    values = jax.random.normal(own_key, shape, jnp.float32) * spread * loudness
    return jnp.minimum(jnp.maximum(values, -most), most).astype(kind)


def setup_inputs(seed: int = 0) -> dict:
    seeds = jax.random.split(jax.random.key(seed), 33)
    return {
        "tokens": normal_values(seeds[0], (GROUPS, SEQ, D), 1.0, 6.0, ((0, 4), (1, 8))),
        "layer_input": normal_values(seeds[1], (GROUPS, SEQ, PLI), 1.0, 6.0, ((0, 4), (1, 8))),
        "prefix_len": touch_ends(jax.random.randint(seeds[2], (GROUPS,), 0, SEQ + 1), jax.random.fold_in(seeds[2], 1), 0, SEQ).astype(jnp.int32),
        "out_grad": normal_values(seeds[3], (GROUPS, SEQ, D), 1.0, 6.0, ((0, 4), (1, 8))),
        "w_attn": normal_values(seeds[4], (D, 2, (QPT + 1) * HD), D ** -0.5, 0.1875, ((0, 4), (1, 2))),
        "w_proj": normal_values(seeds[5], (2, QPT * HD, D), (HEADS * HD) ** -0.5, 0.1875, ((0, 2), (2, 4))),
        "w_gate": normal_values(seeds[6], (D, 2, FF), D ** -0.5, 0.1875, ((0, 4), (2, 2))),
        "w_down": normal_values(seeds[7], (FF, D), FF ** -0.5, 0.078125, ((0, 2), (1, 4))),
        "w_left": normal_values(seeds[8], (D, RANK + PLI), D ** -0.5, 0.1875, ((0, 4),)),
        "w_right": draw_w_right(jax.random.fold_in(seeds[32], 71), 0),
        "w_norm": jnp.clip(1.0 + 0.59375 * jax.random.uniform(seeds[10], (2, HD), jnp.float32) ** block_levels(seeds[10], (2, HD), ((1, 4),), -0.2, 0.2), 1.0, 1.59375).astype(jnp.bfloat16),
        "first_attn": normal_values(seeds[11], (GROUPS, D, 2, (QPT + 1) * HD), 10.0, 60.0, ((0, 4), (1, 4), (2, 2)), jnp.float32),
        "second_attn": jnp.clip(jnp.exp(math.log(1000.0) - 2.3025851 * jax.random.uniform(seeds[12], (GROUPS, D, 2, (QPT + 1) * HD), jnp.float32) ** block_levels(seeds[12], (GROUPS, D, 2, (QPT + 1) * HD), ((0, 4), (1, 4), (2, 2)), -0.2, 0.2)), 100.0, 1000.0),
        "drift_attn": normal_values(seeds[13], (D, 2, (QPT + 1) * HD), 0.01, 0.06, ((0, 4), (1, 2)), jnp.float32),
        "first_proj": normal_values(seeds[14], (GROUPS, 2, QPT * HD, D), 10.0, 60.0, ((0, 4), (1, 2), (3, 4)), jnp.float32),
        "second_proj": jnp.clip(jnp.exp(math.log(1000.0) - 2.3025851 * jax.random.uniform(seeds[15], (GROUPS, 2, QPT * HD, D), jnp.float32) ** block_levels(seeds[15], (GROUPS, 2, QPT * HD, D), ((0, 4), (1, 2), (3, 4)), -0.2, 0.2)), 100.0, 1000.0),
        "drift_proj": normal_values(seeds[16], (2, QPT * HD, D), 0.01, 0.06, ((0, 2), (2, 4)), jnp.float32),
        "first_gate": normal_values(seeds[17], (GROUPS, D, 2, FF), 10.0, 60.0, ((0, 4), (1, 4), (3, 2)), jnp.float32),
        "second_gate": jnp.clip(jnp.exp(math.log(25.0) - 2.5257286 * jax.random.uniform(seeds[18], (GROUPS, D, 2, FF), jnp.float32) ** block_levels(seeds[18], (GROUPS, D, 2, FF), ((0, 4), (1, 4), (3, 2)), -0.2, 0.2)), 2.0, 25.0),
        "drift_gate": normal_values(seeds[19], (D, 2, FF), 0.01, 0.06, ((0, 4), (2, 2)), jnp.float32),
        "first_down": normal_values(seeds[20], (GROUPS, FF, D), 10.0, 60.0, ((0, 4), (1, 2), (2, 4)), jnp.float32),
        "second_down": jnp.clip(jnp.exp(math.log(1000.0) - 2.3025851 * jax.random.uniform(seeds[21], (GROUPS, FF, D), jnp.float32) ** block_levels(seeds[21], (GROUPS, FF, D), ((0, 4), (1, 2), (2, 4)), -0.2, 0.2)), 100.0, 1000.0),
        "drift_down": normal_values(seeds[22], (FF, D), 0.01, 0.06, ((0, 2), (1, 4)), jnp.float32),
        "first_left": normal_values(seeds[23], (GROUPS, D, RANK + PLI), 10.0, 60.0, ((0, 4), (1, 8)), jnp.float32),
        "second_left": jnp.clip(jnp.exp(math.log(1000.0) - 2.3025851 * jax.random.uniform(seeds[24], (GROUPS, D, RANK + PLI), jnp.float32) ** block_levels(seeds[24], (GROUPS, D, RANK + PLI), ((0, 4), (1, 8)), -0.2, 0.2)), 100.0, 1000.0),
        "drift_left": normal_values(seeds[25], (D, RANK + PLI), 0.01, 0.06, ((0, 8),), jnp.float32),
        "first_right": normal_values(seeds[26], (GROUPS, RANK + PLI + 6, D), 10.0, 60.0, ((0, 4), (2, 8)), jnp.float32),
        "second_right": jnp.clip(jnp.exp(math.log(1000.0) - 2.3025851 * jax.random.uniform(seeds[27], (GROUPS, RANK + PLI + 6, D), jnp.float32) ** block_levels(seeds[27], (GROUPS, RANK + PLI + 6, D), ((0, 4), (2, 8)), -0.2, 0.2)), 100.0, 1000.0),
        "drift_right": normal_values(seeds[28], (RANK + PLI + 6, D), 0.01, 0.06, ((1, 8),), jnp.float32),
        "first_norm": normal_values(seeds[29], (GROUPS, 2, HD), 10.0, 60.0, ((0, 4), (2, 8)), jnp.float32),
        "second_norm": jnp.clip(jnp.exp(math.log(1000.0) - 2.3025851 * jax.random.uniform(seeds[30], (GROUPS, 2, HD), jnp.float32) ** block_levels(seeds[30], (GROUPS, 2, HD), ((0, 4), (2, 8)), -0.2, 0.2)), 100.0, 1000.0),
        "drift_norm": normal_values(seeds[31], (2, HD), 0.01, 0.06, ((1, 8),), jnp.float32),
    }


norm_eps = 1e-06
rope_base = 1000000.0
root_two = math.sqrt(2.0)
masked_low = -1e+30
beta_one = 0.9
beta_two = 0.95
adam_eps = 1e-08
learn_rate = 0.01
decay_rate = 0.1
step_count = 10.0
outer_rate = 0.7
outer_keep = 0.9
highest = lax.Precision.HIGHEST

@jax.custom_vjp
def low(v):
    return lax.optimization_barrier(v.astype(jnp.bfloat16)).astype(jnp.float32)

@jax.custom_vjp
def low_back(v):
    return v

def low_keep(v):
    return (low(v), None)

def low_pass(kept, grad):
    return (grad,)

def back_keep(v):
    return (v, None)

def back_low(kept, grad):
    return (low(grad),)
low.defvjp(low_keep, low_pass)
low_back.defvjp(back_keep, back_low)

def matmul(first_op, second_op):
    return jnp.dot(first_op, second_op, precision=highest)

def rms_norm(values_in):
    return values_in * lax.rsqrt(lax.optimization_barrier(jnp.mean(values_in * values_in, axis=-1, keepdims=True)) + norm_eps)

def gelu_tanh(values_in):
    return jax.nn.gelu(values_in, approximate=True)

def rotate(values_in, positions):
    half_size = values_in.shape[-1] // 2
    inverse = rope_base ** (-(jnp.arange(half_size, dtype=jnp.float32) * 2.0 / values_in.shape[-1]))
    angles = positions[:, None] * inverse[None, :]
    shape_out = (angles.shape[0],) + (1,) * (values_in.ndim - 2) + (half_size,)
    cosine = jnp.cos(angles).reshape(shape_out)
    sine_vals = jnp.sin(angles).reshape(shape_out)
    first_half = values_in[..., :half_size]
    second_half = values_in[..., half_size:]
    return jnp.concatenate([first_half * cosine - second_half * sine_vals, second_half * cosine + first_half * sine_vals], axis=-1)

def forward(params, tokens, layer_input, prefix_len):
    w_attn, w_proj, w_gate, w_down, w_left, w_right, w_norm = params
    gain_rows = w_right[RANK + PLI:]
    normed = low(rms_norm(tokens) * gain_rows[0])
    down_rank = low_back(low(matmul(normed, w_left[:, :RANK])))
    up_rank = low_back(matmul(down_rank, w_right[:RANK]))
    laurel = normed + rms_norm(up_rank) * gain_rows[1]
    qkv_proj = low_back(matmul(normed, w_attn.reshape(D, 2 * (QPT + 1) * HD))).reshape(SEQ, 2, QPT + 1, HD)
    positions = jnp.arange(SEQ, dtype=jnp.float32)
    queries = low(rotate(rms_norm(qkv_proj[:, :, :QPT]) * w_norm[0], positions))
    key_vecs = low(rotate(rms_norm(qkv_proj[:, 0, QPT]) * w_norm[1], positions))
    values = low(rms_norm(qkv_proj[:, 1, QPT]))
    query_heads = queries.reshape(SEQ, HEADS, HD).transpose(1, 0, 2)
    spot_index = jnp.arange(SEQ)
    visible = (spot_index[None, :] <= spot_index[:, None]) | (spot_index[None, :] < prefix_len)
    score_scale = HD ** (-0.5)

    def one_head(query_one):
        scores = low_back(matmul(query_one, key_vecs.T) * score_scale)
        scores = jnp.where(visible, scores, masked_low)
        expo_vals = jnp.exp(scores - lax.optimization_barrier(jnp.max(scores, axis=1, keepdims=True)))
        probs = low(expo_vals / lax.optimization_barrier(jnp.sum(expo_vals, axis=1, keepdims=True)))
        return matmul(probs, values)
    mixed = lax.map(jax.checkpoint(one_head), query_heads)
    mixed = low_back(low(mixed.transpose(1, 0, 2).reshape(SEQ, 2, QPT * HD)))
    attn_out = low_back(jnp.einsum('skc,kcd->sd', mixed, w_proj, precision=highest))
    middle = (tokens + rms_norm(attn_out) * gain_rows[2] + laurel) / root_two
    ff_in = low(rms_norm(middle) * gain_rows[3])
    gate_up = low_back(matmul(ff_in, w_gate.reshape(D, 2 * FF))).reshape(SEQ, 2, FF)
    hidden = low(gelu_tanh(gate_up[:, 0]) * gate_up[:, 1])
    ff_out = low_back(matmul(hidden, w_down))
    after_ff = middle + rms_norm(ff_out) * gain_rows[4]
    layer_gate = low_back(matmul(low(after_ff), w_left[:, RANK:]))
    gated = low(gelu_tanh(layer_gate) * layer_input)
    layer_out = low_back(matmul(gated, w_right[RANK:RANK + PLI]))
    return after_ff + rms_norm(layer_out) * gain_rows[5]

def update_one(grad_in, first_in, second, drift_in, weight):
    mean_new = beta_one * first_in + (1 - beta_one) * grad_in
    square_new = beta_two * second + (1 - beta_two) * grad_in * grad_in
    step_size = learn_rate * (mean_new / (1 - beta_one ** step_count) / (jnp.sqrt(square_new / (1 - beta_two ** step_count)) + adam_eps) + decay_rate * weight)
    delta_mean = lax.optimization_barrier(jnp.mean(step_size, axis=0))
    outer_new = outer_keep * drift_in + delta_mean
    master = weight - outer_rate * (delta_mean + outer_keep * outer_new)
    return (mean_new, square_new, delta_mean, outer_new, master)

def reference(tokens, layer_input, prefix_len, out_grad, w_attn, w_proj, w_gate, w_down, w_left, w_right, w_norm, first_attn, second_attn, drift_attn, first_proj, second_proj, drift_proj, first_gate, second_gate, drift_gate, first_down, second_down, drift_down, first_left, second_left, drift_left, first_right, second_right, drift_right, first_norm, second_norm, drift_norm):
    params = (w_attn.astype(jnp.float32), w_proj.astype(jnp.float32), w_gate.astype(jnp.float32), w_down.astype(jnp.float32), w_left.astype(jnp.float32), w_right.astype(jnp.float32), w_norm.astype(jnp.float32))

    def per_group(operands):
        token_one, layer_one, prefix_one, grad_one = operands
        result, pull = jax.vjp(lambda param_set, token_set: forward(param_set, token_set, layer_one, prefix_one), params, token_one)
        param_grads, token_grad = pull(grad_one)
        return (result.astype(jnp.bfloat16), token_grad, param_grads)
    block_out, input_grad, grads = lax.map(per_group, (tokens.astype(jnp.float32), layer_input.astype(jnp.float32), prefix_len, out_grad.astype(jnp.float32)))
    attn_set = update_one(grads[0], first_attn, second_attn, drift_attn, params[0])
    proj_set = update_one(grads[1], first_proj, second_proj, drift_proj, params[1])
    gate_set = update_one(grads[2], first_gate, second_gate, drift_gate, params[2])
    down_set = update_one(grads[3], first_down, second_down, drift_down, params[3])
    left_set = update_one(grads[4], first_left, second_left, drift_left, params[4])
    right_set = update_one(grads[5], first_right, second_right, drift_right, params[5])
    norm_set = update_one(grads[6], first_norm, second_norm, drift_norm, params[6])
    return (block_out, input_grad, grads[0], attn_set[0], attn_set[1], attn_set[2], attn_set[3], attn_set[4], grads[1], proj_set[0], proj_set[1], proj_set[2], proj_set[3], proj_set[4], grads[2], gate_set[0], gate_set[1], gate_set[2], gate_set[3], gate_set[4], grads[3], down_set[0], down_set[1], down_set[2], down_set[3], down_set[4], grads[4], left_set[0], left_set[1], left_set[2], left_set[3], left_set[4], grads[5], right_set[0], right_set[1], right_set[2], right_set[3], grads[6], norm_set[0], norm_set[1], norm_set[2], norm_set[3])
```

```python
import math

import jax
import jax.numpy as jnp
from jax import lax
from jax.sharding import PartitionSpec as P

RANK = 64
PLI = 256


norm_eps = 1e-06
rope_base = 1000000.0
root_two = math.sqrt(2.0)
masked_low = -1e30
beta_one = 0.9
beta_two = 0.95
adam_eps = 1e-08
learn_rate = 0.01
decay_rate = 0.1
step_count = 10.0
outer_rate = 0.7
outer_keep = 0.9
BF = jnp.bfloat16
F32 = jnp.float32


def matmul(first_op, second_op):
    return jnp.dot(first_op, second_op, preferred_element_type=jnp.float32)


def inner_last(first_op, second_op):
    return lax.dot_general(
        first_op, second_op, (((1,), (1,)), ((), ())), preferred_element_type=jnp.float32
    )


def outer_rows(first_op, second_op):
    return lax.dot_general(
        first_op, second_op, (((0,), (0,)), ((), ())), preferred_element_type=jnp.float32
    )


def take_rows(array_in, start, count):
    return lax.dynamic_slice_in_dim(array_in, start, count, 0)


def pick(array_in, index):
    return lax.dynamic_index_in_dim(array_in, index, 0, keepdims=False)


def place(array_in, block, index):
    return lax.dynamic_update_index_in_dim(array_in, block, index, 0)


def rms_norm(values_in):
    return values_in * lax.rsqrt(jnp.mean(values_in * values_in, axis=-1, keepdims=True) + norm_eps)


def scaled_norm(values_in, gain_in):
    return rms_norm(values_in) * gain_in


def norm_back(values_in, gain_in, cotangent):
    unused, pull = jax.vjp(scaled_norm, values_in, gain_in)
    return pull(cotangent)


def gelu_tanh(values_in):
    return jax.nn.gelu(values_in, approximate=True)


def rotate(values_in, positions):
    half_size = values_in.shape[-1] // 2
    inverse = rope_base ** (-(jnp.arange(half_size, dtype=jnp.float32) * 2.0 / values_in.shape[-1]))
    angles = positions[:, None] * inverse[None, :]
    shape_out = (angles.shape[0],) + (1,) * (values_in.ndim - 2) + (half_size,)
    cosine = jnp.cos(angles).reshape(shape_out)
    sine_vals = jnp.sin(angles).reshape(shape_out)
    first_half = values_in[..., :half_size]
    second_half = values_in[..., half_size:]
    return jnp.concatenate(
        [
            first_half * cosine - second_half * sine_vals,
            second_half * cosine + first_half * sine_vals,
        ],
        axis=-1,
    )


def shift(array_in, step):
    size = lax.axis_size("fsdp")
    return lax.ppermute(array_in, "fsdp", [(i, (i + step) % size) for i in range(size)])


def swap(array_in):
    return lax.ppermute(array_in, "tp", [(0, 1), (1, 0)])


def flip(array_in, mask):
    size = lax.axis_size("group")
    return lax.ppermute(array_in, "group", [(i, i ^ mask) for i in range(size)])


def ring_gather(block):
    blocks = [block]
    for unused in range(lax.axis_size("fsdp") - 1):
        blocks.append(shift(blocks[-1], 1))
    return blocks


def ring_sum(part_of):
    size = lax.axis_size("fsdp")
    moving = None
    for step in range(1, size):
        part = part_of(step)
        if moving is not None:
            part = part + moving.astype(F32)
        moving = shift(part.astype(BF), 1)
    return part_of(0) + moving.astype(F32)


def add_groups(array_in, masks):
    total = array_in
    for mask in masks:
        low_total = total.astype(BF)
        total = low_total.astype(F32) + flip(low_total, mask).astype(F32)
    return total


def add_groups_split(array_in, first_mask, second_mask):
    group_index = lax.axis_index("group")
    sides = [(group_index // mask) % 2 for mask in (first_mask, second_mask)]
    part = array_in
    for side, mask in zip(sides, (first_mask, second_mask)):
        half = part.shape[0] // 2
        keep = take_rows(part, side * half, half)
        give = take_rows(part, (1 - side) * half, half)
        part = (keep.astype(F32) + flip(give, mask).astype(F32)).astype(BF)
    for side, mask in zip(sides[::-1], (second_mask, first_mask)):
        other = flip(part, mask)
        part = jnp.where(
            side == 0, jnp.concatenate([part, other], 0), jnp.concatenate([other, part], 0)
        )
    return part.astype(F32)


def share_gather(own_rows, blocks_out):
    size = lax.axis_size("fsdp")
    groups = lax.axis_size("group")
    index = lax.axis_index("fsdp")
    group_index = lax.axis_index("group")
    arrived = [shift(blocks_out(step), step) for step in range(1, size)]
    rows, width = own_rows.shape
    quarter = rows // groups
    full = jnp.zeros((size, groups, quarter, width), own_rows.dtype)
    full = place(full, own_rows.reshape(groups, quarter, width), index)
    for step in range(1, size):
        target = (index + size - step) % size
        for mask in range(groups):
            piece = arrived[step - 1] if mask == 0 else flip(arrived[step - 1], mask)
            full = lax.dynamic_update_slice(
                full, piece[None, None], (target, group_index ^ mask, 0, 0)
            )
    return full.reshape(size * rows, width)


def adam_step(grad_in, first_in, second, weight):
    mean_new = beta_one * first_in + (1 - beta_one) * grad_in
    square_new = beta_two * second + (1 - beta_two) * grad_in * grad_in
    step_size = learn_rate * (
        mean_new
        / (1 - beta_one**step_count)
        / (jnp.sqrt(square_new / (1 - beta_two**step_count)) + adam_eps)
        + decay_rate * weight
    )
    return (mean_new, square_new, step_size)


def per_device(
    tokens,
    layer_input,
    prefix_len,
    out_grad,
    w_attn,
    w_proj,
    w_gate,
    w_down,
    w_left,
    w_right,
    w_norm,
    first_attn,
    second_attn,
    drift_attn,
    first_proj,
    second_proj,
    drift_proj,
    first_gate,
    second_gate,
    drift_gate,
    first_down,
    second_down,
    drift_down,
    first_left,
    second_left,
    drift_left,
    first_right,
    second_right,
    drift_right,
    first_norm,
    second_norm,
    drift_norm,
):
    row_count = tokens.shape[1]
    model_width = tokens.shape[2]
    size = lax.axis_size("fsdp")
    groups = lax.axis_size("group")
    index = lax.axis_index("fsdp")
    tp_index = lax.axis_index("tp")
    group_index = lax.axis_index("group")
    block_rows = row_count * 2
    seq_len = block_rows * size
    head_size = w_norm.shape[1] * size
    per_tp = w_attn.shape[2] // head_size - 1
    query_width = per_tp * head_size
    score_scale = head_size ** (-0.5)
    shard_rows = w_attn.shape[0]
    quarter = shard_rows // groups
    hidden_tp = w_down.shape[0]
    slice_width = -(-hidden_tp // (size * 128)) * 128
    norm_width = w_norm.shape[1]

    attn_rows_w = w_attn[:, 0]
    proj_rows_w = w_proj[0].T
    down_rows_w = w_down.T
    right_rows_w = w_right.T

    small = jnp.concatenate(
        [w_right[RANK + PLI :], jnp.pad(w_norm, ((0, 0), (0, shard_rows - norm_width)))], 0
    )
    small_all = jnp.zeros((size,) + small.shape, BF)
    small_all = place(small_all, small, index)
    for step in range(1, size):
        small_all = place(small_all, shift(small, step), (index + size - step) % size)
    small_all = small_all.astype(F32)
    gain_rows = small_all[:, :6].transpose(1, 0, 2).reshape(6, model_width)
    gain_pair = small_all[:, 6:, :norm_width].transpose(1, 0, 2).reshape(2, head_size)

    side_w = jnp.zeros((size, shard_rows, head_size), BF)
    for step, block in enumerate(ring_gather(attn_rows_w[:, query_width:])):
        side_w = place(side_w, block, (index + size - step) % size)
    side_w = side_w.reshape(model_width, head_size)

    query_own = attn_rows_w[:, :query_width]
    query_part = take_rows(query_own, group_index * quarter, quarter)
    query_w = share_gather(query_own, lambda step: query_part)

    residual = tokens[0].astype(F32)
    normed_b = (rms_norm(residual) * gain_rows[0]).astype(BF)
    normed_other = swap(normed_b)
    normed_all = jnp.where(
        tp_index == 0,
        jnp.concatenate([normed_b, normed_other], 0),
        jnp.concatenate([normed_other, normed_b], 0),
    )
    positions = (index * block_rows + jnp.arange(block_rows)).astype(F32)

    def side_map(side_in, gain_in):
        plain = rms_norm(side_in)
        return jnp.where(tp_index == 0, rotate(plain * gain_in, positions), plain)

    def query_map(query_in, gain_in):
        return rotate(rms_norm(query_in) * gain_in, positions)

    side_proj = matmul(normed_all, side_w)
    side_rows = side_map(side_proj, gain_pair[1]).astype(BF)
    key_list = []
    value_list = []
    pos_list = []
    for step, own_side in enumerate(ring_gather(side_rows)):
        other_side = swap(own_side)
        key_list.append(jnp.where(tp_index == 0, own_side, other_side))
        value_list.append(jnp.where(tp_index == 0, other_side, own_side))
        pos_list.append((index + size - step) % size * block_rows + jnp.arange(block_rows))
    key_all = jnp.concatenate(key_list, 0)
    value_all = jnp.concatenate(value_list, 0)
    key_pos = jnp.concatenate(pos_list, 0)
    query_proj = matmul(normed_all, query_w).reshape(block_rows, per_tp, head_size)
    queries = query_map(query_proj, gain_pair[0]).astype(BF)
    row_pos = index * block_rows + jnp.arange(block_rows)
    seen = (key_pos[None, :] <= row_pos[:, None]) | (key_pos[None, :] < prefix_len[0])

    rest_own = jnp.concatenate(
        [proj_rows_w, w_left[:, RANK:], right_rows_w[:, RANK : RANK + PLI], w_left[:, :RANK], right_rows_w[:, :RANK]],
        1,
    )
    rest_part = take_rows(rest_own, group_index * quarter, quarter)
    rest_w = share_gather(rest_own, lambda step: rest_part)
    width = proj_rows_w.shape[1]
    proj_w = rest_w[:, :width]
    left_gate_w = rest_w[:, width : width + PLI]
    right_proj_w = rest_w[:, width + PLI : width + 2 * PLI]
    left_rank_w = rest_w[:, width + 2 * PLI : width + 2 * PLI + RANK]
    right_rank_w = rest_w[:, width + 2 * PLI + RANK :]

    def hidden_slice(rows_in, which):
        low_end = min(which * slice_width, hidden_tp)
        high_end = min(low_end + slice_width, hidden_tp)
        cut = rows_in[:, low_end:high_end]
        return jnp.pad(cut, ((0, 0), (0, slice_width - (high_end - low_end))))

    def hidden_block(gate_in, down_in, which):
        pieces = [
            jnp.concatenate(
                [
                    hidden_slice(gate_in[:, 0], j),
                    hidden_slice(gate_in[:, 1], j),
                    hidden_slice(down_in, j),
                ],
                1,
            )
            for j in range(size)
        ]
        chosen = pieces[0]
        for j in range(1, size):
            chosen = jnp.where(which == j, pieces[j], chosen)
        return chosen

    gate_part = take_rows(w_gate, group_index * quarter, quarter)
    down_part = take_rows(down_rows_w, group_index * quarter, quarter)
    ff_w = share_gather(
        hidden_block(w_gate, down_rows_w, index),
        lambda step: hidden_block(gate_part, down_part, (index + step) % size),
    )
    gate_w = ff_w[:, : 2 * slice_width]
    down_w = ff_w[:, 2 * slice_width :]

    mixed_list = []
    log_list = []
    for head in range(per_tp):
        scores = jnp.where(seen, inner_last(queries[:, head], key_all) * score_scale, masked_low)
        row_top = jnp.max(scores, axis=1, keepdims=True)
        expo_vals = jnp.exp(scores - row_top)
        row_total = jnp.sum(expo_vals, axis=1, keepdims=True)
        probs_b = (expo_vals / row_total).astype(BF)
        mixed_list.append(matmul(probs_b, value_all).astype(BF))
        log_list.append(row_top + jnp.log(row_total))
    mixed_rows = jnp.concatenate(mixed_list, 1)

    def tp_sum(part):
        keep = take_rows(part, tp_index * row_count, row_count)
        give = take_rows(part, (1 - tp_index) * row_count, row_count)
        return keep + swap(give.astype(BF)).astype(F32)

    attn_rows = tp_sum(inner_last(mixed_rows, proj_w))

    normed_f = normed_b.astype(F32)
    rank_down = matmul(normed_b, left_rank_w).astype(BF)
    rank_up = inner_last(rank_down, right_rank_w)
    laurel = normed_f + rms_norm(rank_up) * gain_rows[1]
    middle = (residual + rms_norm(attn_rows) * gain_rows[2] + laurel) / root_two
    ff_in = (rms_norm(middle) * gain_rows[3]).astype(BF)

    def pair_rows(own):
        return jnp.concatenate([own, swap(own)], 0)

    def pair_sum(part):
        return part[:row_count] + swap(part[row_count:].astype(BF)).astype(F32)

    ff_blocks = []
    gate_up_blocks = []
    hidden_blocks = []
    out_parts = []
    moving = None
    current = ff_in
    for step in range(size):
        if step:
            current = shift(current, 1)
        ff_block = pair_rows(current)
        gate_up = matmul(ff_block, gate_w)
        hidden = (gelu_tanh(gate_up[:, :slice_width]) * gate_up[:, slice_width:]).astype(BF)
        part = pair_sum(inner_last(hidden, down_w))
        if step == 0:
            own_part = part
        else:
            if moving is not None:
                part = part + moving.astype(F32)
            moving = shift(part.astype(BF), 1)
        ff_blocks.append(ff_block)
        gate_up_blocks.append(gate_up)
        hidden_blocks.append(hidden)
    ff_out = own_part + moving.astype(F32)

    after_ff = middle + rms_norm(ff_out) * gain_rows[4]
    after_b = after_ff.astype(BF)
    layer_gate = matmul(after_b, left_gate_w)
    side_input = layer_input[0].astype(F32)
    gated = (gelu_tanh(layer_gate) * side_input).astype(BF)
    layer_out = inner_last(gated, right_proj_w)
    block_out = (after_ff + rms_norm(layer_out) * gain_rows[5]).astype(BF)

    out_cot = out_grad[0].astype(F32)
    d_layer, gain_five = norm_back(layer_out, gain_rows[5], out_cot)
    d_layer_b = d_layer.astype(BF)
    grad_layer_proj = outer_rows(d_layer_b, gated)
    d_gated = matmul(d_layer_b, right_proj_w)
    unused, gate_pull = jax.vjp(lambda gate_in: gelu_tanh(gate_in) * side_input, layer_gate)
    d_gate_in = gate_pull(d_gated)[0].astype(BF)
    grad_layer_gate = outer_rows(after_b, d_gate_in)
    d_after = out_cot + inner_last(d_gate_in, left_gate_w)
    d_ff, gain_four = norm_back(ff_out, gain_rows[4], d_after)
    current = d_ff.astype(BF)
    d_ff_blocks = []
    d_gate_up_blocks = []
    moving = None
    for step in range(size):
        if step:
            current = shift(current, 1)
        d_ff_block = pair_rows(current)
        d_hidden = matmul(d_ff_block, down_w)
        unused, glu_pull = jax.vjp(
            lambda gate_in, up_in: gelu_tanh(gate_in) * up_in,
            gate_up_blocks[step][:, :slice_width],
            gate_up_blocks[step][:, slice_width:],
        )
        d_gate_up = jnp.concatenate([v.astype(BF) for v in glu_pull(d_hidden)], 1)
        part = pair_sum(inner_last(d_gate_up, gate_w))
        if step == 0:
            own_part = part
        else:
            if moving is not None:
                part = part + moving.astype(F32)
            moving = shift(part.astype(BF), 1)
        d_ff_blocks.append(d_ff_block)
        d_gate_up_blocks.append(d_gate_up)
    d_ff_in = own_part + moving.astype(F32)

    grad_down_w = outer_rows(jnp.concatenate(d_ff_blocks, 0), jnp.concatenate(hidden_blocks, 0))
    grad_gate_w = outer_rows(jnp.concatenate(ff_blocks, 0), jnp.concatenate(d_gate_up_blocks, 0))

    def to_shards(grad_in):
        blocks = grad_in.astype(BF).reshape(size, shard_rows, grad_in.shape[1])
        arrived = [pick(blocks, index)]
        for step in range(1, size):
            arrived.append(shift(pick(blocks, (index + step) % size), step))
        stacked = jnp.stack(arrived, 0)
        return [pick(stacked, (index + size - j) % size) for j in range(size)]

    down_pieces = to_shards(grad_down_w)
    gate_pieces = to_shards(grad_gate_w)
    grad_down = jnp.concatenate(down_pieces, 1)[:, :hidden_tp]
    grad_gate = jnp.stack(
        [
            jnp.concatenate([p[:, :slice_width] for p in gate_pieces], 1)[:, :hidden_tp],
            jnp.concatenate([p[:, slice_width:] for p in gate_pieces], 1)[:, :hidden_tp],
        ],
        1,
    )

    d_mid_norm, gain_three = norm_back(middle, gain_rows[3], d_ff_in)
    d_middle = d_after + d_mid_norm
    d_share = d_middle / root_two
    d_attn, gain_two = norm_back(attn_rows, gain_rows[2], d_share)
    d_attn_b = d_attn.astype(BF)
    d_attn_other = swap(d_attn_b)
    d_attn_all = jnp.where(
        tp_index == 0,
        jnp.concatenate([d_attn_b, d_attn_other], 0),
        jnp.concatenate([d_attn_other, d_attn_b], 0),
    )
    d_mixed = matmul(d_attn_all, proj_w).astype(BF)
    grad_proj_w = outer_rows(d_attn_all, mixed_rows)

    d_key_all = jnp.zeros((seq_len, head_size), F32)
    d_value_all = jnp.zeros((seq_len, head_size), F32)
    d_query_list = []
    for head in range(per_tp):
        query_one = queries[:, head]
        grad_one = d_mixed[:, head * head_size : (head + 1) * head_size]
        scores = jnp.where(seen, inner_last(query_one, key_all) * score_scale, masked_low)
        probs = jnp.exp(scores - log_list[head])
        probs_b = probs.astype(BF)
        d_probs = inner_last(grad_one, value_all)
        row_dot = jnp.sum(d_probs * probs, axis=1, keepdims=True)
        d_scores = (probs * (d_probs - row_dot)).astype(BF)
        d_query_list.append(matmul(d_scores, key_all) * score_scale)
        d_key_all = d_key_all + outer_rows(d_scores, query_one) * score_scale
        d_value_all = d_value_all + outer_rows(probs_b, grad_one)
    own_grad = jnp.where(tp_index == 0, d_key_all, d_value_all)
    give_grad = jnp.where(tp_index == 0, d_value_all, d_key_all)
    side_grad = own_grad + swap(give_grad.astype(BF)).astype(F32)
    side_grad = side_grad.reshape(size, block_rows, head_size)
    d_side_rows = ring_sum(lambda step: side_grad[step])
    d_query = jnp.stack(d_query_list, 1)

    unused, query_pull = jax.vjp(query_map, query_proj, gain_pair[0])
    d_query_proj, norm_zero = query_pull(d_query)
    unused, side_pull = jax.vjp(side_map, side_proj, gain_pair[1])
    d_side_proj, norm_one = side_pull(d_side_rows)
    d_query_b = d_query_proj.reshape(block_rows, query_width).astype(BF)
    d_side_b = d_side_proj.astype(BF)
    d_qkv_b = jnp.concatenate([d_query_b, d_side_b], 1)
    grad_attn_w = outer_rows(normed_all, d_qkv_b)
    d_normed_attn = tp_sum(inner_last(d_query_b, query_w) + inner_last(d_side_b, side_w))
    d_rank_up, gain_one = norm_back(rank_up, gain_rows[1], d_share)
    d_rank_up_b = d_rank_up.astype(BF)
    grad_rank_up = outer_rows(d_rank_up_b, rank_down)
    d_rank_down = matmul(d_rank_up_b, right_rank_w).astype(BF)
    grad_rank_down = outer_rows(normed_b, d_rank_down)
    d_normed = d_share + inner_last(d_rank_down, left_rank_w) + d_normed_attn
    d_input, gain_zero = norm_back(residual, gain_rows[0], d_normed)
    input_grad = d_share + d_input

    grad_mid = jnp.concatenate([grad_attn_w, grad_proj_w], 1).reshape(size, shard_rows, -1)
    grad_mid = ring_sum(lambda step: pick(grad_mid, (index + size - step) % size)).astype(BF)
    gain_grads = jnp.stack(
        [gain_zero, gain_one, gain_two, gain_three, gain_four, gain_five], axis=1
    )
    half_rows = shard_rows // 2
    grad_lr = jnp.concatenate(
        [grad_rank_down, grad_layer_gate, grad_rank_up, grad_layer_proj, gain_grads], 1
    )
    lr_width = grad_lr.shape[1]
    half_norm = norm_width // 2
    norm_grads = jnp.stack([norm_zero, norm_one], 0).reshape(2, size, 2, half_norm)
    norm_grads = norm_grads.transpose(1, 2, 0, 3).reshape(size, 2, 1, 2 * half_norm)
    norm_grads = jnp.pad(norm_grads, ((0, 0), (0, 0), (0, 0), (0, lr_width - 2 * half_norm)))
    grad_lr = jnp.concatenate([grad_lr.reshape(size, 2, half_rows, lr_width), norm_grads], 2)
    keep_lr = lax.dynamic_index_in_dim(grad_lr, tp_index, 1, keepdims=False)
    give_lr = lax.dynamic_index_in_dim(grad_lr, 1 - tp_index, 1, keepdims=False)
    grad_lr = keep_lr + swap(give_lr.astype(BF)).astype(F32)
    grad_lr = ring_sum(lambda step: pick(grad_lr, (index + size - step) % size)).astype(BF)

    grad_list = (
        grad_mid[:, : w_attn.shape[2]].astype(F32)[:, None],
        grad_mid[:, w_attn.shape[2] :].astype(F32).T[None],
        grad_gate.astype(F32),
        grad_down.astype(F32).T,
        grad_lr[:half_rows, : RANK + PLI].astype(F32),
        grad_lr[:half_rows, RANK + PLI :].astype(F32).T,
        grad_lr[half_rows, : 2 * half_norm].astype(F32).reshape(2, half_norm),
    )
    left_part = w_left.shape[0] // 2
    right_part = w_right.shape[1] // 2
    norm_part = w_norm.shape[1] // 2
    old_list = (
        w_attn.astype(F32),
        w_proj.astype(F32),
        w_gate.astype(F32),
        w_down.astype(F32),
        take_rows(w_left, tp_index * left_part, left_part).astype(F32),
        lax.dynamic_slice_in_dim(w_right, tp_index * right_part, right_part, 1).astype(F32),
        lax.dynamic_slice_in_dim(w_norm, tp_index * norm_part, norm_part, 1).astype(F32),
    )
    first_list = (
        first_attn[0],
        first_proj[0],
        first_gate[0],
        first_down[0],
        first_left[0],
        first_right[0],
        first_norm[0],
    )
    second_list = (
        second_attn[0],
        second_proj[0],
        second_gate[0],
        second_down[0],
        second_left[0],
        second_right[0],
        second_norm[0],
    )
    drift_list = (
        drift_attn,
        drift_proj,
        drift_gate,
        drift_down,
        drift_left,
        drift_right,
        drift_norm,
    )
    mean_list = []
    square_list = []
    step_list = []
    for which in range(7):
        mean_new, square_new, step_size = adam_step(
            grad_list[which], first_list[which], second_list[which], old_list[which]
        )
        mean_list.append(mean_new)
        square_list.append(square_new)
        step_list.append(step_size.astype(BF))

    def total_large(step_in):
        half = step_in.shape[0] // 2
        return jnp.concatenate(
            [add_groups_split(step_in[:half], 1, 2), add_groups_split(step_in[half:], 2, 1)], 0
        )

    if groups == 4:
        lr_step = jnp.concatenate([step_list[4], step_list[5].T], 1)
        norm_step = jnp.pad(
            step_list[6].reshape(1, -1), ((0, 0), (0, lr_width - 2 * half_norm))
        )
        lr_sum = add_groups(jnp.concatenate([lr_step, norm_step], 0), (2, 1))
        step_sums = (
            add_groups(step_list[0][:, 0], (1, 2))[:, None],
            add_groups(step_list[1][0].T, (2, 1)).T[None],
            total_large(step_list[2]),
            total_large(step_list[3].T).T,
            lr_sum[:half_rows, : RANK + PLI],
            lr_sum[:half_rows, RANK + PLI :].T,
            lr_sum[half_rows, : 2 * half_norm].reshape(2, half_norm),
        )
    else:
        step_sums = [lax.psum(step_one, "group").astype(F32) for step_one in step_list]
    results = [block_out[None], input_grad[None]]
    for which in range(7):
        delta_mean = step_sums[which] / groups
        outer_new = outer_keep * drift_list[which] + delta_mean
        results.extend(
            [
                grad_list[which][None],
                mean_list[which][None],
                square_list[which][None],
                delta_mean,
                outer_new,
            ]
        )
        if which < 5:
            master = old_list[which] - outer_rate * (delta_mean + outer_keep * outer_new)
            results.append(master)
    return tuple(results)


def solution(mesh):
    placed = (
        P("group", ("fsdp", "tp"), None),
        P("group", ("fsdp", "tp"), None),
        P("group"),
        P("group", ("fsdp", "tp"), None),
        P("fsdp", "tp", None),
        P("tp", None, "fsdp"),
        P("fsdp", None, "tp"),
        P("tp", "fsdp"),
        P("fsdp", None),
        P(None, "fsdp"),
        P(None, "fsdp"),
        P("group", "fsdp", "tp", None),
        P("group", "fsdp", "tp", None),
        P("fsdp", "tp", None),
        P("group", "tp", None, "fsdp"),
        P("group", "tp", None, "fsdp"),
        P("tp", None, "fsdp"),
        P("group", "fsdp", None, "tp"),
        P("group", "fsdp", None, "tp"),
        P("fsdp", None, "tp"),
        P("group", "tp", "fsdp"),
        P("group", "tp", "fsdp"),
        P("tp", "fsdp"),
        P("group", ("fsdp", "tp"), None),
        P("group", ("fsdp", "tp"), None),
        P(("fsdp", "tp"), None),
        P("group", None, ("fsdp", "tp")),
        P("group", None, ("fsdp", "tp")),
        P(None, ("fsdp", "tp")),
        P("group", None, ("fsdp", "tp")),
        P("group", None, ("fsdp", "tp")),
        P(None, ("fsdp", "tp")),
    )
    return jax.shard_map(
        per_device,
        mesh=mesh,
        in_specs=placed,
        out_specs=(
            P("group", ("fsdp", "tp"), None),
            P("group", ("fsdp", "tp"), None),
            P("group", "fsdp", "tp", None),
            P("group", "fsdp", "tp", None),
            P("group", "fsdp", "tp", None),
            P("fsdp", "tp", None),
            P("fsdp", "tp", None),
            P("fsdp", "tp", None),
            P("group", "tp", None, "fsdp"),
            P("group", "tp", None, "fsdp"),
            P("group", "tp", None, "fsdp"),
            P("tp", None, "fsdp"),
            P("tp", None, "fsdp"),
            P("tp", None, "fsdp"),
            P("group", "fsdp", None, "tp"),
            P("group", "fsdp", None, "tp"),
            P("group", "fsdp", None, "tp"),
            P("fsdp", None, "tp"),
            P("fsdp", None, "tp"),
            P("fsdp", None, "tp"),
            P("group", "tp", "fsdp"),
            P("group", "tp", "fsdp"),
            P("group", "tp", "fsdp"),
            P("tp", "fsdp"),
            P("tp", "fsdp"),
            P("tp", "fsdp"),
            P("group", ("fsdp", "tp"), None),
            P("group", ("fsdp", "tp"), None),
            P("group", ("fsdp", "tp"), None),
            P(("fsdp", "tp"), None),
            P(("fsdp", "tp"), None),
            P(("fsdp", "tp"), None),
            P("group", None, ("fsdp", "tp")),
            P("group", None, ("fsdp", "tp")),
            P("group", None, ("fsdp", "tp")),
            P(None, ("fsdp", "tp")),
            P(None, ("fsdp", "tp")),
            P("group", None, ("fsdp", "tp")),
            P("group", None, ("fsdp", "tp")),
            P("group", None, ("fsdp", "tp")),
            P(None, ("fsdp", "tp")),
            P(None, ("fsdp", "tp")),
        ),
        check_vma=False,
    )
```
